32 devices in a mesh: col: 8 (over z, y), lev: 4 (over x, core).
Axes of the slice: x: 2, y: 2, z: 4, core: 2. Of those that a mesh axis runs over, the one named last changes fastest.
Arguments:
- state_anom: bfloat16 [48, 64, 8192], P('lev', None, 'col'), may hold values from -6 to 6
- error_sum: float32 [48, 8192], P('lev', 'col'), may hold values from -3 to 3
- obs_anom: bfloat16 [64, 16384], P('lev', 'col'), may hold values from -6 to 6
- local_weight: float32 [32, 16384], P(None, 'col'), may hold values from 0.05 to 1
- neighbours: int32 [32, 16384], P(None, 'col'), may hold values from 0 to 3071, as said below
- innovation: float32 [16384], P(('col', 'lev')), may hold values from -6 to 6
- obs_type: int32 [16384], P(('col', 'lev')), may hold values from 0 to 31
- live: int32 [16384], P(('col', 'lev')), may hold values 0 or 1
Outputs:
- impact: float32 [16384], P(('col', 'lev'))
- type_impact: float32 [32], replicated
The draws below stay inside these ranges and needn't reach their ends.
Inputs may be any that keep to these rules, and one draw needn't show every extreme that they name: Observation o lies in column tile o // 2048; the column (o // 2048 - 1) * 1024 + neighbours[n, o] lies in that tile or the tile on either side of it, inside the grid.
All inputs are finite; a program needn't handle non-finite values. No bound on the sum of `live` on one device may be relied on, other than what follows from the above.
Results may differ from the reference program's by a relative error of at most 0.0003.
Values may be sent and summed in bfloat16 or wider, within the bound.
A program may use at most 64 MiB of HBM per device.

```python
import jax
import jax.numpy as jnp
from jax import lax

MEMBERS = 64
LEV = 48
NEIGH = 32
BLOCK = 128
NTYPE = 32
COL_DEV = 1024
BLK_DEV = 16
COLS = 8192
OBS_DEV = 2048
OBS = 16384
N_COL = 8


def draw_neighbours(key, part):
    slots = jnp.arange(OBS, dtype=jnp.int32)
    tile = slots // OBS_DEV
    base = (tile - 1) * COL_DEV
    lower = jnp.maximum(tile - 1, 0) * COL_DEV - base
    upper = jnp.minimum(tile + 2, N_COL) * COL_DEV - base
    lower = jnp.broadcast_to(lower[None, :], (NEIGH, OBS))
    upper = jnp.broadcast_to(upper[None, :], (NEIGH, OBS))
    return jax.random.randint(jax.random.fold_in(key, 11), (NEIGH, OBS), lower, upper, dtype=jnp.int32)


def place_ends(array, own_key, low, top_value):
    index_at = [jax.random.randint(jax.random.fold_in(own_key, axis), (), 0, length) for axis, length in enumerate(array.shape)]
    widest = array.shape.index(max(array.shape))
    next_to = index_at[:widest] + [(index_at[widest] + 1) % array.shape[widest]] + index_at[widest + 1:]
    return array.at[tuple(index_at)].set(low).at[tuple(next_to)].set(top_value)


def shard_levels(stream_key, shape, split, least, high):
    level = 1.0
    for position, blocks in split:
        draws = jax.random.uniform(jax.random.fold_in(jax.random.fold_in(stream_key, 6), position), (blocks,), jnp.float32, least / len(split), high / len(split))
        level = level * jnp.repeat(jnp.exp(draws), shape[position] // blocks).reshape((-1,) + (1,) * (len(shape) - 1 - position))
    return level


def noise(rng, dims, scale, reach, cuts=(), kind=jnp.bfloat16):
    entries = jax.random.normal(rng, dims, jnp.float32) * scale
    if len(cuts) > 0:
        entries = shard_levels(rng, dims, cuts, -0.22, 0.18) * entries
    return jnp.clip(entries, min=-reach, max=reach).astype(kind)


def setup_inputs(seed: int = 0) -> dict:
    arg_keys = jax.random.split(jax.random.key(seed), 9)
    state_anom = noise(arg_keys[0], (LEV, MEMBERS, COLS), 1.0, 6.0, ((0, 4), (2, 8)))
    error_sum = noise(arg_keys[1], (LEV, COLS), 0.2, 3.0, ((0, 4), (1, 8)), jnp.float32)
    obs_anom = noise(arg_keys[2], (MEMBERS, OBS), 1.0, 6.0, ((0, 4), (1, 8)))
    local_weight = jnp.clip(0.05 + 0.95 * jax.random.uniform(arg_keys[3], (NEIGH, OBS), jnp.float32) ** shard_levels(arg_keys[3], (NEIGH, OBS), ((1, 8),), -0.2, 0.2), 0.05, 1.0)
    neighbours = draw_neighbours(jax.random.fold_in(arg_keys[8], 71), 0)
    innovation = noise(arg_keys[5], (OBS,), 1.0, 6.0, ((0, 32),), jnp.float32)
    obs_type = place_ends(jax.random.randint(arg_keys[6], (OBS,), 0, NTYPE), jax.random.fold_in(arg_keys[6], 1), 0, NTYPE - 1).astype(jnp.int32)
    live = place_ends((jax.random.randint(arg_keys[7], (OBS,), 0, 4) < 3).astype(jnp.int32), jax.random.fold_in(arg_keys[7], 1), 0, 1)
    return {"state_anom": state_anom, "error_sum": error_sum, "obs_anom": obs_anom, "local_weight": local_weight, "neighbours": neighbours, "innovation": innovation, "obs_type": obs_type, "live": live}


def reference(state_anom, error_sum, obs_anom, local_weight, neighbours, innovation, obs_type, live):
    sens = jnp.einsum("lkc,lc->kc", state_anom.astype(jnp.float32), error_sum, precision=lax.Precision.HIGHEST)
    step_rows = BLOCK * BLK_DEV
    count = OBS // step_rows
    anom_blocks = jnp.transpose(obs_anom.reshape(MEMBERS, count, step_rows), (1, 0, 2))
    weight_blocks = jnp.transpose(local_weight.reshape(NEIGH, count, step_rows), (1, 0, 2))
    index_blocks = jnp.transpose(neighbours.reshape(NEIGH, count, step_rows), (1, 0, 2))
    tile_ids = jnp.arange(count, dtype=jnp.int32)

    def one_block(items):
        anom, weight, index, tile = items
        start = ((tile - 1) * COL_DEV).astype(jnp.int32)
        picked = jnp.take(sens, (index + start).astype(jnp.int32), axis=1)
        spread = jnp.einsum("kno,no->ko", picked, weight, precision=lax.Precision.HIGHEST)
        return jnp.sum(anom.astype(jnp.float32) * spread, axis=0)

    pair = lax.map(one_block, (anom_blocks, weight_blocks, index_blocks, tile_ids)).reshape(OBS)
    impact = pair * innovation * live.astype(jnp.float32) / (MEMBERS - 1.0)
    onehot = (obs_type[None, :] == jnp.arange(NTYPE, dtype=jnp.int32)[:, None]).astype(jnp.float32)
    type_impact = jnp.sum(onehot * impact[None, :], axis=1)
    return impact, type_impact
```

```python
import functools

import jax
import jax.numpy as jnp
from jax import lax
from jax.experimental import pallas as pl
from jax.experimental.pallas import tpu as pltpu
from jax.sharding import PartitionSpec as P

MEMBERS = 64
NTYPE = 32
LANES = 128
MESH = pl.DeviceIdType.MESH


def remote(src, dst, send, recv, target):
    return pltpu.make_async_remote_copy(
        src_ref=src, dst_ref=dst, send_sem=send, recv_sem=recv, device_id=target, device_id_type=MESH
    )


def kernel(
    dims,
    state_hbm, error_hbm, anom_hbm, weight_hbm, index_hbm, innov_hbm, type_hbm, live_hbm,
    impact_ref, total_ref,
    state, error, part, landed, sens, anom, anom_t, weight, index, index_t, innov, kind, live,
    split, table, picked, pair_out, pair_in, type_out, type_in,
    load_sem, quarter_sem, list_sem, anom_sem, own_sem,
    rs_send, rs_recv, an_send, an_recv, me_send, me_recv, ga_send, ga_recv,
    ha_send, ha_recv, fw_send, fw_recv, pa_send, pa_recv, ty_send, ty_recv,
):
    ncol, nlev, nlo, nhi, groups = dims
    quarter = impact_ref.shape[0] * impact_ref.shape[1]
    rows_q = impact_ref.shape[0]
    mq = anom_hbm.shape[0]
    neigh = index_hbm.shape[0]
    go = quarter // rows_q
    columns = state.shape[2]
    levels = state.shape[0]
    hpt = columns // LANES
    total = ncol * nlev

    col = lax.axis_index("col")
    lev = lax.axis_index("lev")
    hi = lev // nlo
    lo = lev % nlo
    me = col * nlev + lev

    copy_err = pltpu.make_async_copy(error_hbm, error, load_sem.at[0])
    copy_err.start()
    state_loads = []
    for d in range(1, nlev + 1):
        q = lax.rem(lev + d, nlev)
        rows = pl.ds(pl.multiple_of(q * mq, mq), mq)
        c = pltpu.make_async_copy(state_hbm.at[:, rows, :], state.at[:, rows, :], quarter_sem.at[d - 1])
        c.start()
        state_loads.append(c)
    list_loads = []
    for g in range(groups):
        h = (g * go) // quarter
        start = (h * nlo + lo) * quarter + (g * go) % quarter
        cols = pl.ds(pl.multiple_of(start, go), go)
        for i, (src, dst) in enumerate(((index_hbm, index), (weight_hbm, weight))):
            c = pltpu.make_async_copy(src.at[:, cols], dst.at[pl.ds(g * neigh, neigh), :], list_sem.at[i, g])
            c.start()
            list_loads.append(c)
    own_loads = []
    for h in range(nhi):
        cols = pl.ds(pl.multiple_of((h * nlo + lo) * quarter, quarter), quarter)
        c = pltpu.make_async_copy(
            anom_hbm.at[:, cols], anom.at[lo, :, pl.ds(h * quarter, quarter)], anom_sem.at[h]
        )
        c.start()
        own_loads.append(c)
    for i, (src, dst) in enumerate(((innov_hbm, innov), (type_hbm, kind), (live_hbm, live))):
        c = pltpu.make_async_copy(src, dst.at[hi], own_sem.at[i])
        c.start()
        own_loads.append(c)

    barrier = pltpu.get_barrier_semaphore()

    def greet(d, carry):
        p = lax.rem(me + d, total)
        pl.semaphore_signal(
            barrier, inc=1, device_id={"col": p // nlev, "lev": lax.rem(p, nlev)}, device_id_type=MESH
        )
        return carry

    lax.fori_loop(1, total, greet, 0)

    copy_err.wait()
    for d in range(1, nlev + 1):
        q = lax.rem(lev + d, nlev)
        rows = pl.ds(pl.multiple_of(q * mq, mq), mq)
        state_loads[d - 1].wait()
        acc = state[0, rows, :].astype(jnp.float32) * error[pl.ds(0, 1), :]
        for l in range(1, levels):
            acc = acc + state[l, rows, :].astype(jnp.float32) * error[pl.ds(l, 1), :]
        part[d - 1] = acc

    pl.semaphore_wait(barrier, total - 1)

    scatter = []
    for d in range(1, nlev):
        q = lax.rem(lev + d, nlev)
        c = remote(part.at[d - 1], landed.at[d - 1], rs_send.at[d - 1], rs_recv.at[d - 1], {"lev": q})
        c.start()
        scatter.append(c)
    anom_sends = []
    for d in range(1, nlo):
        other = lax.rem(lo + d, nlo)
        for h in range(nhi):
            cols = pl.ds(pl.multiple_of((h * nlo + other) * quarter, quarter), quarter)
            c = remote(
                anom_hbm.at[:, cols], anom.at[lo, :, pl.ds(h * quarter, quarter)],
                an_send.at[d - 1, h], an_recv.at[d - 1, h], {"lev": hi * nlo + other},
            )
            c.start()
            anom_sends.append(c)
    meta_sends = []
    for d in range(1, nhi):
        other = lax.rem(hi + d, nhi)
        for i, (src, dst) in enumerate(((innov_hbm, innov), (type_hbm, kind), (live_hbm, live))):
            c = remote(src, dst.at[hi], me_send.at[d - 1, i], me_recv.at[d - 1, i], {"lev": other * nlo + lo})
            c.start()
            meta_sends.append(c)

    for c in list_loads:
        c.wait()
    index_t[...] = index[...].T
    picked[...] = jnp.zeros_like(picked)

    for c in scatter:
        c.wait_recv()
    summed = part[nlev - 1]
    for d in range(1, nlev):
        summed = summed + landed[d - 1]
    sens[1, lo] = summed

    left = {"col": jnp.maximum(col - 1, 0)}
    right = {"col": jnp.minimum(col + 1, ncol - 1)}
    to_left = remote(sens.at[1, lo], sens.at[2, lo], ha_send.at[0], ha_recv.at[1], left)
    to_right = remote(sens.at[1, lo], sens.at[0, lo], ha_send.at[1], ha_recv.at[0], right)
    has_left = col > 0
    has_right = col < ncol - 1
    pl.when(has_left)(to_left.start)
    pl.when(has_right)(to_right.start)
    gather = []
    for d in range(1, nlo):
        other = lax.rem(lo + d, nlo)
        c = remote(sens.at[1, lo], sens.at[1, lo], ga_send.at[d - 1], ga_recv.at[d - 1], {"lev": hi * nlo + other})
        c.start()
        gather.append(c)

    for c in own_loads:
        c.wait()
    for c in anom_sends:
        c.wait_recv()
    members = nlo * mq
    parts = 3
    depth = anom_t.shape[1]
    flat = anom[...].reshape(members, anom.shape[2]).astype(jnp.float32)
    pieces = [flat] * parts
    if depth > parts * members:
        pieces.append(jnp.zeros((depth - parts * members, anom.shape[2]), jnp.float32))
        split[pl.ds(parts * members, depth - parts * members), :] = jnp.zeros(
            (depth - parts * members, columns), jnp.bfloat16
        )
    anom_t[...] = jnp.concatenate(pieces, axis=0).T.astype(jnp.bfloat16)

    lane_group = lax.broadcasted_iota(jnp.int32, (8, LANES), 1) // neigh

    def tile(j):
        rest = sens[j].reshape(members, columns)
        for i in range(parts):
            piece = rest.astype(jnp.bfloat16)
            split[pl.ds(i * members, members), :] = piece
            rest = rest - piece.astype(jnp.float32)
        for g in range(groups):
            table[g % 2] = jnp.dot(
                anom_t[pl.ds(g * go, go), :], split[...], preferred_element_type=jnp.float32
            )

            def pick(r, carry):
                for u in range(4):
                    rows = pl.ds(pl.multiple_of(r * 32 + u * 8, 8), 8)
                    where = index_t[rows, :]
                    lane = where & (LANES - 1)
                    block = jnp.where(lane_group == g, where >> 7, -1)
                    acc = picked[rows, :]
                    for h in range(hpt):
                        got = jnp.take_along_axis(
                            table[g % 2, rows, pl.ds(h * LANES, LANES)], lane, axis=1, mode="promise_in_bounds"
                        )
                        acc = jnp.where(block == j * hpt + h, got, acc)
                    picked[rows, :] = acc
                return carry

            lax.fori_loop(0, go // 32, pick, 0)

    for c in gather:
        c.wait_recv()
    tile(1)

    forwards = []
    for side, here in ((0, has_left), (2, has_right)):
        copies = []
        for d in range(1, nlo):
            other = lax.rem(lo + d, nlo)
            copies.append(
                remote(
                    sens.at[side, lo], sens.at[side, lo], fw_send.at[d - 1, side // 2],
                    fw_recv.at[d - 1, side // 2], {"lev": hi * nlo + other},
                )
            )
        forwards.append((side, here, copies))
    for side, here, copies in forwards:
        @pl.when(here)
        def _():
            (to_right if side == 0 else to_left).wait_recv()
            for c in copies:
                c.start()
    for side, here, copies in forwards:
        @pl.when(here)
        def _():
            for c in copies:
                c.wait_recv()
            tile(side)

    pair = (picked[...].T * weight[...]).reshape(groups, neigh, go).sum(axis=1)
    pair_out[...] = pair.reshape(nhi, rows_q, go)
    pair_sends = []
    for d in range(1, nhi):
        other = lax.rem(hi + d, nhi)
        c = remote(
            pair_out.at[other], pair_in.at[d - 1], pa_send.at[d - 1], pa_recv.at[d - 1], {"lev": other * nlo + lo}
        )
        c.start()
        pair_sends.append(c)

    for c in meta_sends:
        c.wait_recv()
    ids = lax.broadcasted_iota(jnp.int32, (NTYPE, go), 0)
    binned = jnp.zeros((NTYPE, go), jnp.float32)
    for h in range(nhi):
        share = pair_out[h] * innov[h] * live[h].astype(jnp.float32) / (MEMBERS - 1.0)
        kinds = kind[h]
        for r in range(rows_q):
            binned = binned + jnp.where(ids == kinds[r:r + 1, :], share[r:r + 1, :], 0.0)
    folded = binned[:, :LANES]
    for b in range(1, go // LANES):
        folded = folded + binned[:, b * LANES:(b + 1) * LANES]
    square = jnp.concatenate([folded, jnp.zeros((LANES - NTYPE, LANES), jnp.float32)], axis=0)
    type_row = jnp.sum(square.T, axis=0, keepdims=True)
    type_out[...] = type_row
    type_in[me] = type_row

    def spread(d, carry):
        p = lax.rem(me + d, total)
        remote(
            type_out, type_in.at[me], ty_send.at[0], ty_recv.at[0], {"col": p // nlev, "lev": lax.rem(p, nlev)}
        ).start()
        return carry

    lax.fori_loop(1, total, spread, 0)

    for c in pair_sends:
        c.wait_recv()
    whole = pair_out[hi]
    for d in range(1, nhi):
        whole = whole + pair_in[d - 1]
    impact_ref[...] = whole * innov[hi] * live[hi].astype(jnp.float32) / (MEMBERS - 1.0)

    everyone = remote(
        type_in.at[pl.ds(0, total - 1)], type_in.at[pl.ds(0, total - 1)], ty_send.at[0], ty_recv.at[0], {"lev": lev}
    )
    everyone.wait_recv()
    total_ref[...] = jnp.sum(type_in[...], axis=0)

    for c in scatter + anom_sends + meta_sends + gather + pair_sends:
        c.wait_send()
    pl.when(has_left)(to_left.wait_send)
    pl.when(has_right)(to_right.wait_send)
    for side, here, copies in forwards:
        @pl.when(here)
        def _():
            for c in copies:
                c.wait_send()
    everyone.wait_send()


def shards(state_anom, error_sum, obs_anom, local_weight, neighbours, innovation, obs_type, live):
    ncol, nlev = lax.axis_size("col"), lax.axis_size("lev")
    nlo = 2 if nlev % 2 == 0 else 1
    nhi = nlev // nlo
    levels, members, columns = state_anom.shape
    mq, obs_slots = obs_anom.shape
    neigh = local_weight.shape[0]
    quarter = innovation.shape[0]
    handled = quarter * nhi
    groups = LANES // neigh
    go = handled // groups
    rows_q = quarter // go
    half = nlo * mq
    depth = -(-3 * half // LANES) * LANES
    total = ncol * nlev
    dma = pltpu.SemaphoreType.DMA
    f32, bf16, i32 = jnp.float32, jnp.bfloat16, jnp.int32
    vm = pltpu.VMEM
    scratch = [
        vm((levels, members, columns), bf16), vm((levels, columns), f32), vm((nlev, mq, columns), f32),
        vm((max(nlev - 1, 1), mq, columns), f32), vm((3, nlo, mq, columns), f32), vm((nlo, mq, handled), bf16),
        vm((handled, depth), bf16), vm((LANES, go), f32), vm((LANES, go), i32), vm((go, LANES), i32),
        vm((nhi, rows_q, go), f32), vm((nhi, rows_q, go), i32), vm((nhi, rows_q, go), i32),
        vm((depth, columns), bf16), vm((2, go, columns), f32), vm((go, LANES), f32),
        vm((nhi, rows_q, go), f32), vm((max(nhi - 1, 1), rows_q, go), f32),
        vm((1, LANES), f32), vm((total, 1, LANES), f32),
        dma((1,)), dma((nlev,)), dma((2, groups)), dma((nhi,)), dma((3,)),
        dma((nlev,)), dma((nlev,)), dma((nlo, nhi)), dma((nlo, nhi)), dma((nhi, 3)), dma((nhi, 3)),
        dma((nlo,)), dma((nlo,)), dma((2,)), dma((2,)), dma((nlo, 2)), dma((nlo, 2)),
        dma((nhi,)), dma((nhi,)), dma((1,)), dma((1,)),
    ]
    anywhere = pl.BlockSpec(memory_space=pl.ANY)
    impact, totals = pl.pallas_call(
        functools.partial(kernel, (ncol, nlev, nlo, nhi, groups)),
        out_shape=(jax.ShapeDtypeStruct((rows_q, go), f32), jax.ShapeDtypeStruct((1, LANES), f32)),
        in_specs=[anywhere] * 8,
        out_specs=(pl.BlockSpec(memory_space=pltpu.VMEM), pl.BlockSpec(memory_space=pltpu.VMEM)),
        scratch_shapes=scratch,
        compiler_params=pltpu.CompilerParams(collective_id=0, has_side_effects=True),
    )(
        state_anom, error_sum, obs_anom, local_weight, neighbours,
        innovation.reshape(rows_q, go), obs_type.reshape(rows_q, go), live.reshape(rows_q, go),
    )
    return impact.reshape(quarter), totals[0, :NTYPE]


def solution(mesh):
    in_specs = (
        P("lev", None, "col"),
        P("lev", "col"),
        P("lev", "col"),
        P(None, "col"),
        P(None, "col"),
        P(("col", "lev")),
        P(("col", "lev")),
        P(("col", "lev")),
    )
    out_specs = (P(("col", "lev")), P())
    return jax.shard_map(shards, mesh=mesh, in_specs=in_specs, out_specs=out_specs, check_vma=False)
```

```python
import functools

import jax
import jax.numpy as jnp
from jax import lax
from jax.experimental import pallas as pl
from jax.experimental.pallas import tpu as pltpu
from jax.sharding import PartitionSpec as P

MEMBERS = 64
NTYPE = 32
LANES = 128
MESH = pl.DeviceIdType.MESH


def remote(src, dst, send, recv, target):
    return pltpu.make_async_remote_copy(
        src_ref=src, dst_ref=dst, send_sem=send, recv_sem=recv, device_id=target, device_id_type=MESH
    )


def kernel(
    dims,
    state_hbm, error_hbm, anom_hbm, weight_hbm, index_hbm, innov_hbm, type_hbm, live_hbm,
    impact_ref, total_ref,
    state, error, part, landed, sens, anom, anom_t, weight, index, index_t, innov, kind, live,
    split, table, picked, pair_out, pair_in, type_out, type_in,
    load_sem, quarter_sem, list_sem, anom_sem, own_sem,
    rs_send, rs_recv, an_send, an_recv, me_send, me_recv, ga_send, ga_recv,
    ha_send, ha_recv, fw_send, fw_recv, pa_send, pa_recv, ty_send, ty_recv,
):
    ncol, nlev, nlo, nhi, groups = dims
    quarter = impact_ref.shape[1]
    mq = anom_hbm.shape[0]
    neigh = index_hbm.shape[0]
    go = index.shape[1]
    rows_q = quarter // go
    columns = state.shape[2]
    levels = state.shape[0]
    hpt = columns // LANES
    total = ncol * nlev

    col = lax.axis_index("col")
    lev = lax.axis_index("lev")
    hi = lev // nlo
    lo = lev % nlo
    me = col * nlev + lev

    copy_err = pltpu.make_async_copy(error_hbm, error, load_sem.at[0])
    copy_err.start()
    state_loads = []
    for d in range(1, nlev + 1):
        q = lax.rem(lev + d, nlev)
        rows = pl.ds(pl.multiple_of(q * mq, mq), mq)
        c = pltpu.make_async_copy(state_hbm.at[:, rows, :], state.at[:, rows, :], quarter_sem.at[d - 1])
        c.start()
        state_loads.append(c)
    list_loads = []
    for g in range(groups):
        h = (g * go) // quarter
        start = (h * nlo + lo) * quarter + (g * go) % quarter
        cols = pl.ds(pl.multiple_of(start, go), go)
        for i, (src, dst) in enumerate(((index_hbm, index), (weight_hbm, weight))):
            c = pltpu.make_async_copy(src.at[:, cols], dst.at[pl.ds(g * neigh, neigh), :], list_sem.at[i, g])
            c.start()
            list_loads.append(c)
    own_loads = []
    for h in range(nhi):
        cols = pl.ds(pl.multiple_of((h * nlo + lo) * quarter, quarter), quarter)
        c = pltpu.make_async_copy(
            anom_hbm.at[:, cols], anom.at[lo, :, pl.ds(h * quarter, quarter)], anom_sem.at[h]
        )
        c.start()
        own_loads.append(c)
    for i, (src, dst) in enumerate(((innov_hbm, innov), (type_hbm, kind), (live_hbm, live))):
        c = pltpu.make_async_copy(src, dst.at[hi], own_sem.at[i])
        c.start()
        own_loads.append(c)

    barrier = pltpu.get_barrier_semaphore()

    def greet(d, carry):
        p = lax.rem(me + d, total)
        pl.semaphore_signal(
            barrier, inc=1, device_id={"col": p // nlev, "lev": lax.rem(p, nlev)}, device_id_type=MESH
        )
        return carry

    lax.fori_loop(1, total, greet, 0)

    copy_err.wait()
    for d in range(1, nlev + 1):
        q = lax.rem(lev + d, nlev)
        rows = pl.ds(pl.multiple_of(q * mq, mq), mq)
        state_loads[d - 1].wait()
        acc = state[0, rows, :].astype(jnp.float32) * error[pl.ds(0, 1), :]
        for l in range(1, levels):
            acc = acc + state[l, rows, :].astype(jnp.float32) * error[pl.ds(l, 1), :]
        part[d - 1] = acc

    pl.semaphore_wait(barrier, total - 1)

    scatter = []
    for d in range(1, nlev):
        q = lax.rem(lev + d, nlev)
        c = remote(part.at[d - 1], landed.at[d - 1], rs_send.at[d - 1], rs_recv.at[d - 1], {"lev": q})
        c.start()
        scatter.append(c)
    anom_sends = []
    for d in range(1, nlo):
        other = lax.rem(lo + d, nlo)
        for h in range(nhi):
            cols = pl.ds(pl.multiple_of((h * nlo + other) * quarter, quarter), quarter)
            c = remote(
                anom_hbm.at[:, cols], anom.at[lo, :, pl.ds(h * quarter, quarter)],
                an_send.at[d - 1, h], an_recv.at[d - 1, h], {"lev": hi * nlo + other},
            )
            c.start()
            anom_sends.append(c)
    meta_sends = []
    for d in range(1, nhi):
        other = lax.rem(hi + d, nhi)
        for i, (src, dst) in enumerate(((innov_hbm, innov), (type_hbm, kind), (live_hbm, live))):
            c = remote(src, dst.at[hi], me_send.at[d - 1, i], me_recv.at[d - 1, i], {"lev": other * nlo + lo})
            c.start()
            meta_sends.append(c)

    for c in list_loads:
        c.wait()
    index_t[...] = index[...].T
    picked[...] = jnp.zeros_like(picked)

    for c in scatter:
        c.wait_recv()
    summed = part[nlev - 1]
    for d in range(1, nlev):
        summed = summed + landed[d - 1]
    sens[1, lo] = summed

    left = {"col": jnp.maximum(col - 1, 0)}
    right = {"col": jnp.minimum(col + 1, ncol - 1)}
    to_left = remote(sens.at[1, lo], sens.at[2, lo], ha_send.at[0], ha_recv.at[1], left)
    to_right = remote(sens.at[1, lo], sens.at[0, lo], ha_send.at[1], ha_recv.at[0], right)
    has_left = col > 0
    has_right = col < ncol - 1
    pl.when(has_left)(to_left.start)
    pl.when(has_right)(to_right.start)
    gather = []
    for d in range(1, nlo):
        other = lax.rem(lo + d, nlo)
        c = remote(sens.at[1, lo], sens.at[1, lo], ga_send.at[d - 1], ga_recv.at[d - 1], {"lev": hi * nlo + other})
        c.start()
        gather.append(c)

    for c in own_loads:
        c.wait()
    for c in anom_sends:
        c.wait_recv()
    members = nlo * mq
    parts = 3
    depth = anom_t.shape[1]
    flat = anom[...].reshape(members, anom.shape[2]).astype(jnp.float32)
    pieces = [flat] * parts
    if depth > parts * members:
        pieces.append(jnp.zeros((depth - parts * members, anom.shape[2]), jnp.float32))
        split[pl.ds(parts * members, depth - parts * members), :] = jnp.zeros(
            (depth - parts * members, columns), jnp.bfloat16
        )
    anom_t[...] = jnp.concatenate(pieces, axis=0).T.astype(jnp.bfloat16)

    lane_group = lax.broadcasted_iota(jnp.int32, (8, LANES), 1) // neigh

    def tile(j):
        rest = sens[j].reshape(members, columns)
        for i in range(parts):
            piece = rest.astype(jnp.bfloat16)
            split[pl.ds(i * members, members), :] = piece
            rest = rest - piece.astype(jnp.float32)
        for g in range(groups):
            table[g] = jnp.dot(anom_t[pl.ds(g * go, go), :], split[...], preferred_element_type=jnp.float32)

        def pick(r, carry):
            for u in range(2):
                rows = pl.ds(pl.multiple_of(r * 16 + u * 8, 8), 8)
                where = index_t[rows, :]
                lane = where & (LANES - 1)
                block = where >> 7
                acc = picked[rows, :]
                for g in range(groups):
                    mine = jnp.where(lane_group == g, block, -1)
                    for h in range(hpt):
                        got = jnp.take_along_axis(
                            table[g, rows, pl.ds(h * LANES, LANES)], lane, axis=1, mode="promise_in_bounds"
                        )
                        acc = jnp.where(mine == j * hpt + h, got, acc)
                picked[rows, :] = acc
            return carry

        lax.fori_loop(0, go // 16, pick, 0)

    for c in gather:
        c.wait_recv()
    tile(1)

    forwards = []
    for side, here in ((0, has_left), (2, has_right)):
        copies = []
        for d in range(1, nlo):
            other = lax.rem(lo + d, nlo)
            copies.append(
                remote(
                    sens.at[side, lo], sens.at[side, lo], fw_send.at[d - 1, side // 2],
                    fw_recv.at[d - 1, side // 2], {"lev": hi * nlo + other},
                )
            )
        forwards.append((side, here, copies))
    for side, here, copies in forwards:
        @pl.when(here)
        def _():
            (to_right if side == 0 else to_left).wait_recv()
            for c in copies:
                c.start()
    for side, here, copies in forwards:
        @pl.when(here)
        def _():
            for c in copies:
                c.wait_recv()
            tile(side)

    pair = (picked[...].T * weight[...]).reshape(groups, neigh, go).sum(axis=1)
    for h in range(nhi):
        pair_out[h] = jnp.concatenate([pair[h * rows_q + r:h * rows_q + r + 1] for r in range(rows_q)], axis=1)
    pair_sends = []
    for d in range(1, nhi):
        other = lax.rem(hi + d, nhi)
        c = remote(
            pair_out.at[other], pair_in.at[d - 1], pa_send.at[d - 1], pa_recv.at[d - 1], {"lev": other * nlo + lo}
        )
        c.start()
        pair_sends.append(c)

    for c in meta_sends:
        c.wait_recv()
    ids = lax.broadcasted_iota(jnp.int32, (NTYPE, quarter), 0)
    binned = jnp.zeros((NTYPE, quarter), jnp.float32)
    for h in range(nhi):
        share = pair_out[h] * innov[h] * live[h].astype(jnp.float32) / (MEMBERS - 1.0)
        binned = binned + jnp.where(ids == kind[h], share, 0.0)
    folded = binned[:, :LANES]
    for b in range(1, quarter // LANES):
        folded = folded + binned[:, b * LANES:(b + 1) * LANES]
    square = jnp.concatenate([folded, jnp.zeros((LANES - NTYPE, LANES), jnp.float32)], axis=0)
    type_row = jnp.sum(square.T, axis=0, keepdims=True)
    type_out[...] = type_row
    type_in[me] = type_row

    def spread(d, carry):
        p = lax.rem(me + d, total)
        remote(
            type_out, type_in.at[me], ty_send.at[0], ty_recv.at[0], {"col": p // nlev, "lev": lax.rem(p, nlev)}
        ).start()
        return carry

    lax.fori_loop(1, total, spread, 0)

    for c in pair_sends:
        c.wait_recv()
    whole = pair_out[hi]
    for d in range(1, nhi):
        whole = whole + pair_in[d - 1]
    impact_ref[...] = whole * innov[hi] * live[hi].astype(jnp.float32) / (MEMBERS - 1.0)

    everyone = remote(
        type_in.at[pl.ds(0, total - 1)], type_in.at[pl.ds(0, total - 1)], ty_send.at[0], ty_recv.at[0], {"lev": lev}
    )
    everyone.wait_recv()
    total_ref[...] = jnp.sum(type_in[...], axis=0)

    for c in scatter + anom_sends + meta_sends + gather + pair_sends:
        c.wait_send()
    pl.when(has_left)(to_left.wait_send)
    pl.when(has_right)(to_right.wait_send)
    for side, here, copies in forwards:
        @pl.when(here)
        def _():
            for c in copies:
                c.wait_send()
    everyone.wait_send()


def shards(state_anom, error_sum, obs_anom, local_weight, neighbours, innovation, obs_type, live):
    ncol, nlev = lax.axis_size("col"), lax.axis_size("lev")
    nlo = 2 if nlev % 2 == 0 else 1
    nhi = nlev // nlo
    levels, members, columns = state_anom.shape
    mq, obs_slots = obs_anom.shape
    neigh = local_weight.shape[0]
    quarter = innovation.shape[0]
    handled = quarter * nhi
    groups = LANES // neigh
    go = handled // groups
    half = nlo * mq
    depth = -(-3 * half // LANES) * LANES
    total = ncol * nlev
    dma = pltpu.SemaphoreType.DMA
    f32, bf16, i32 = jnp.float32, jnp.bfloat16, jnp.int32
    vm = pltpu.VMEM
    scratch = [
        vm((levels, members, columns), bf16), vm((levels, columns), f32), vm((nlev, mq, columns), f32),
        vm((max(nlev - 1, 1), mq, columns), f32), vm((3, nlo, mq, columns), f32), vm((nlo, mq, handled), bf16),
        vm((handled, depth), bf16), vm((LANES, go), f32), vm((LANES, go), i32), vm((go, LANES), i32),
        vm((nhi, 1, quarter), f32), vm((nhi, 1, quarter), i32), vm((nhi, 1, quarter), i32),
        vm((depth, columns), bf16), vm((groups, go, columns), f32), vm((go, LANES), f32),
        vm((nhi, 1, quarter), f32), vm((max(nhi - 1, 1), 1, quarter), f32),
        vm((1, LANES), f32), vm((total, 1, LANES), f32),
        dma((1,)), dma((nlev,)), dma((2, groups)), dma((nhi,)), dma((3,)),
        dma((nlev,)), dma((nlev,)), dma((nlo, nhi)), dma((nlo, nhi)), dma((nhi, 3)), dma((nhi, 3)),
        dma((nlo,)), dma((nlo,)), dma((2,)), dma((2,)), dma((nlo, 2)), dma((nlo, 2)),
        dma((nhi,)), dma((nhi,)), dma((1,)), dma((1,)),
    ]
    anywhere = pl.BlockSpec(memory_space=pl.ANY)
    impact, totals = pl.pallas_call(
        functools.partial(kernel, (ncol, nlev, nlo, nhi, groups)),
        out_shape=(jax.ShapeDtypeStruct((1, quarter), f32), jax.ShapeDtypeStruct((1, LANES), f32)),
        in_specs=[anywhere] * 8,
        out_specs=(pl.BlockSpec(memory_space=pltpu.VMEM), pl.BlockSpec(memory_space=pltpu.VMEM)),
        scratch_shapes=scratch,
        compiler_params=pltpu.CompilerParams(collective_id=0, has_side_effects=True),
    )(
        state_anom, error_sum, obs_anom, local_weight, neighbours,
        innovation.reshape(1, quarter), obs_type.reshape(1, quarter), live.reshape(1, quarter),
    )
    return impact.reshape(quarter), totals[0, :NTYPE]


def solution(mesh):
    in_specs = (
        P("lev", None, "col"),
        P("lev", "col"),
        P("lev", "col"),
        P(None, "col"),
        P(None, "col"),
        P(("col", "lev")),
        P(("col", "lev")),
        P(("col", "lev")),
    )
    out_specs = (P(("col", "lev")), P())
    return jax.shard_map(shards, mesh=mesh, in_specs=in_specs, out_specs=out_specs, check_vma=False)
```

```python
import functools

import jax
import jax.numpy as jnp
from jax import lax
from jax.experimental import pallas as pl
from jax.experimental.pallas import tpu as pltpu
from jax.sharding import PartitionSpec as P

MEMBERS = 64
NTYPE = 32
LANES = 128
MESH = pl.DeviceIdType.MESH


def remote(src, dst, send, recv, target):
    return pltpu.make_async_remote_copy(
        src_ref=src, dst_ref=dst, send_sem=send, recv_sem=recv, device_id=target, device_id_type=MESH
    )


def kernel(
    dims,
    state_hbm, error_hbm, anom_hbm, weight_hbm, index_hbm, innov_hbm, type_hbm, live_hbm,
    impact_ref, total_ref,
    state, error, part, landed, sens, anom, anom_t, weight, index, index_t, innov, kind, live,
    split, table, picked, pair_out, pair_in, type_out, type_in,
    word, load_sem, quarter_sem, list_sem, anom_sem, own_sem,
    rs_send, rs_recv, an_send, an_recv, me_send, me_recv, ga_send, ga_recv,
    ha_send, ha_recv, fw_send, fw_recv, pa_send, pa_recv, ty_send, ty_recv,
):
    ncol, nlev, nlo, nhi, groups, chunks = dims
    quarter = impact_ref.shape[1]
    mq = anom_hbm.shape[0]
    neigh = index_hbm.shape[0]
    go = index.shape[1]
    rows_q = quarter // go
    columns = state.shape[2]
    levels = state.shape[0]
    hpt = columns // LANES
    total = ncol * nlev
    width = columns // chunks
    spans = [pl.ds(c * width, width) for c in range(chunks)]

    col = lax.axis_index("col")
    lev = lax.axis_index("lev")
    hi = lev // nlo
    lo = lev % nlo
    me = col * nlev + lev

    def visit(act):
        def one(dc):
            c = col + dc
            c = jnp.where(c >= ncol, c - ncol, c)
            for dl in range(nlev):
                l = lev + dl
                act(c, jnp.where(l >= nlev, l - nlev, l))

        if ncol <= 8:
            for dc in range(ncol - 1, 0, -1):
                one(dc)
        else:
            lax.fori_loop(1, ncol, lambda dc, carry: (one(dc), carry)[1], 0)
        for dl in range(1, nlev):
            l = lev + dl
            act(col, jnp.where(l >= nlev, l - nlev, l))

    barrier = pltpu.get_barrier_semaphore()
    for d in range(1, nlev):
        pl.semaphore_signal(barrier, inc=1, device_id={"lev": lax.rem(lev + d, nlev)}, device_id_type=MESH)

    def hail(sem, reach):
        for here, there in ((col >= reach, col - reach), (col < ncol - reach, col + reach)):
            @pl.when(here)
            def _():
                pl.semaphore_signal(sem, inc=1, device_id={"col": there}, device_id_type=MESH)

    def heard(reach):
        return jnp.where(col >= reach, 1, 0) + jnp.where(col < ncol - reach, 1, 0)

    hail(barrier, 1)
    rounds = max(1, (ncol - 1).bit_length())

    copy_err = pltpu.make_async_copy(error_hbm, error, load_sem.at[0])
    copy_err.start()
    state_loads = []
    for k, span in enumerate(spans):
        c = pltpu.make_async_copy(state_hbm.at[:, :, span], state.at[:, :, span], quarter_sem.at[k])
        c.start()
        state_loads.append(c)
    list_loads = []
    for g in range(groups):
        h = (g * go) // quarter
        start = (h * nlo + lo) * quarter + (g * go) % quarter
        cols = pl.ds(pl.multiple_of(start, go), go)
        for i, (src, dst) in enumerate(((index_hbm, index), (weight_hbm, weight))):
            c = pltpu.make_async_copy(src.at[:, cols], dst.at[pl.ds(g * neigh, neigh), :], list_sem.at[i, g])
            c.start()
            list_loads.append(c)
    own_loads = []
    for h in range(nhi):
        cols = pl.ds(pl.multiple_of((h * nlo + lo) * quarter, quarter), quarter)
        c = pltpu.make_async_copy(
            anom_hbm.at[:, cols], anom.at[lo, :, pl.ds(h * quarter, quarter)], anom_sem.at[h]
        )
        c.start()
        own_loads.append(c)
    for i, (src, dst) in enumerate(((innov_hbm, innov), (type_hbm, kind), (live_hbm, live))):
        c = pltpu.make_async_copy(src, dst.at[hi], own_sem.at[i])
        c.start()
        own_loads.append(c)

    copy_err.wait()
    scatter = []
    for k, span in enumerate(spans):
        state_loads[k].wait()
        for b in range(width // LANES):
            lanes = pl.ds(k * width + b * LANES, LANES)
            acc = state[0, :, lanes].astype(jnp.float32) * error[pl.ds(0, 1), lanes]
            for l in range(1, levels):
                acc = acc + state[l, :, lanes].astype(jnp.float32) * error[pl.ds(l, 1), lanes]
            part[:, :, lanes] = acc.reshape(nlev, mq, LANES)
        if k == 0:
            pl.semaphore_wait(barrier, nlev - 1 + heard(1))
            hail(word.at[0], 1)
        sends = []
        for d in range(1, nlev):
            q = lax.rem(lev + d, nlev)
            c = remote(
                part.at[q, :, span], landed.at[d - 1, :, span], rs_send.at[d - 1, k], rs_recv.at[d - 1, k], {"lev": q}
            )
            c.start()
            sends.append(c)
        scatter.append(sends)
    anom_sends = []
    for d in range(1, nlo):
        other = lax.rem(lo + d, nlo)
        for h in range(nhi):
            cols = pl.ds(pl.multiple_of((h * nlo + other) * quarter, quarter), quarter)
            c = remote(
                anom_hbm.at[:, cols], anom.at[lo, :, pl.ds(h * quarter, quarter)],
                an_send.at[d - 1, h], an_recv.at[d - 1, h], {"lev": hi * nlo + other},
            )
            c.start()
            anom_sends.append(c)
    meta_sends = []
    for d in range(1, nhi):
        other = lax.rem(hi + d, nhi)
        for i, (src, dst) in enumerate(((innov_hbm, innov), (type_hbm, kind), (live_hbm, live))):
            c = remote(src, dst.at[hi], me_send.at[d - 1, i], me_recv.at[d - 1, i], {"lev": other * nlo + lo})
            c.start()
            meta_sends.append(c)

    for c in list_loads:
        c.wait()
    index_t[...] = index[...].T
    picked[...] = jnp.zeros_like(picked)

    left = {"col": jnp.maximum(col - 1, 0)}
    right = {"col": jnp.minimum(col + 1, ncol - 1)}
    has_left = col > 0
    has_right = col < ncol - 1
    partners = [hi * nlo + lax.rem(lo + d, nlo) for d in range(1, nlo)]
    halo = []
    gather = []
    for k, span in enumerate(spans):
        for c in scatter[k]:
            c.wait_recv()
        summed = part[lev, :, span]
        for d in range(1, nlev):
            summed = summed + landed[d - 1, :, span]
        sens[1, lo, :, span] = summed
        mine = sens.at[1, lo, :, span]
        to_left = remote(mine, sens.at[2, lo, :, span], ha_send.at[0, k], ha_recv.at[1, k], left)
        to_right = remote(mine, sens.at[0, lo, :, span], ha_send.at[1, k], ha_recv.at[0, k], right)
        pl.when(has_left)(to_left.start)
        pl.when(has_right)(to_right.start)
        halo.append((to_left, to_right))
        copies = []
        for d, partner in enumerate(partners):
            c = remote(mine, mine, ga_send.at[d, k], ga_recv.at[d, k], {"lev": partner})
            c.start()
            copies.append(c)
        gather.append(copies)

    for c in own_loads:
        c.wait()
    for c in anom_sends:
        c.wait_recv()
    members = nlo * mq
    parts = 3
    depth = anom_t.shape[1]
    flat = anom[...].reshape(members, anom.shape[2]).astype(jnp.float32)
    pieces = [flat] * parts
    if depth > parts * members:
        pieces.append(jnp.zeros((depth - parts * members, anom.shape[2]), jnp.float32))
        split[pl.ds(parts * members, depth - parts * members), :] = jnp.zeros(
            (depth - parts * members, width), jnp.bfloat16
        )
    anom_t[...] = jnp.concatenate(pieces, axis=0).T.astype(jnp.bfloat16)

    lane_group = lax.broadcasted_iota(jnp.int32, (8, LANES), 1) // neigh

    def tile(j, k):
        rest = sens[j, :, :, spans[k]].reshape(members, width)
        for i in range(parts):
            piece = rest.astype(jnp.bfloat16)
            split[pl.ds(i * members, members), :] = piece
            rest = rest - piece.astype(jnp.float32)
        for g in range(groups):
            table[g] = jnp.dot(anom_t[pl.ds(g * go, go), :], split[...], preferred_element_type=jnp.float32)
        first = j * hpt + k * (width // LANES)

        def pick(r, carry):
            for u in range(8):
                rows = pl.ds(pl.multiple_of(r * 64 + u * 8, 8), 8)
                where = index_t[rows, :]
                lane = where & (LANES - 1)
                block = where >> 7
                acc = picked[rows, :]
                for g in range(groups):
                    mine = jnp.where(lane_group == g, block, -1)
                    for h in range(width // LANES):
                        got = jnp.take_along_axis(
                            table[g, rows, pl.ds(h * LANES, LANES)], lane, axis=1, mode="promise_in_bounds"
                        )
                        acc = jnp.where(mine == first + h, got, acc)
                picked[rows, :] = acc
            return carry

        lax.fori_loop(0, go // 64, pick, 0)

    forwards = []
    for k, span in enumerate(spans):
        for side, here in ((0, has_left), (2, has_right)):
            copies = []
            for d, partner in enumerate(partners):
                landing = sens.at[side, lo, :, span]
                copies.append(
                    remote(landing, landing, fw_send.at[d, side, k], fw_recv.at[d, side, k], {"lev": partner})
                )
            forwards.append((side, here, copies, k))

    def forward(k):
        for side, here, copies, at in forwards:
            if at == k:
                @pl.when(here)
                def _():
                    halo[k][1 if side == 0 else 0].wait_recv()
                    for c in copies:
                        c.start()

    def relay(i):
        if i < rounds:
            pl.semaphore_wait(word.at[i], heard(1 << i))
            if i + 1 < rounds:
                hail(word.at[i + 1], 1 << (i + 1))

    relay(0)
    for k in range(chunks):
        for c in gather[k]:
            c.wait_recv()
        tile(1, k)
        forward(k)
    relay(1)
    for side, here, copies, k in forwards:
        @pl.when(here)
        def _():
            for c in copies:
                c.wait_recv()
            tile(side, k)

    for i in range(2, rounds):
        relay(i)

    pair = (picked[...].T * weight[...]).reshape(groups, neigh, go).sum(axis=1)
    for h in range(nhi):
        pair_out[h] = jnp.concatenate([pair[h * rows_q + r:h * rows_q + r + 1] for r in range(rows_q)], axis=1)
    pair_sends = []
    for d in range(1, nhi):
        other = lax.rem(hi + d, nhi)
        c = remote(
            pair_out.at[other], pair_in.at[d - 1], pa_send.at[d - 1], pa_recv.at[d - 1], {"lev": other * nlo + lo}
        )
        c.start()
        pair_sends.append(c)

    for c in meta_sends:
        c.wait_recv()
    ids = lax.broadcasted_iota(jnp.int32, (NTYPE, quarter), 0)
    binned = jnp.zeros((NTYPE, quarter), jnp.float32)
    for h in range(nhi):
        share = pair_out[h] * innov[h] * live[h].astype(jnp.float32) / (MEMBERS - 1.0)
        binned = binned + jnp.where(ids == kind[h], share, 0.0)
    folded = binned[:, :LANES]
    for b in range(1, quarter // LANES):
        folded = folded + binned[:, b * LANES:(b + 1) * LANES]
    square = jnp.concatenate([folded, jnp.zeros((LANES - NTYPE, LANES), jnp.float32)], axis=0)
    type_row = jnp.sum(square.T, axis=0, keepdims=True)
    type_out[...] = type_row
    type_in[me] = type_row

    visit(
        lambda c, l: remote(
            type_out, type_in.at[me], ty_send.at[0], ty_recv.at[0], {"col": c, "lev": l}
        ).start()
    )

    for c in pair_sends:
        c.wait_recv()
    whole = pair_out[hi]
    for d in range(1, nhi):
        whole = whole + pair_in[d - 1]
    impact_ref[...] = whole * innov[hi] * live[hi].astype(jnp.float32) / (MEMBERS - 1.0)

    everyone = remote(
        type_in.at[pl.ds(0, total - 1)], type_in.at[pl.ds(0, total - 1)], ty_send.at[0], ty_recv.at[0], {"lev": lev}
    )
    everyone.wait_recv()
    total_ref[...] = jnp.sum(type_in[...], axis=0)

    for c in sum(scatter + gather, []) + anom_sends + meta_sends + pair_sends:
        c.wait_send()
    for to_left, to_right in halo:
        pl.when(has_left)(to_left.wait_send)
        pl.when(has_right)(to_right.wait_send)
    for side, here, copies, k in forwards:
        @pl.when(here)
        def _():
            for c in copies:
                c.wait_send()
    everyone.wait_send()


def hand_over(impact_in, total_in, impact_ref, total_ref):
    impact_ref[...] = impact_in[...]
    total_ref[...] = total_in[:, :total_ref.shape[1]]


def shards(state_anom, error_sum, obs_anom, local_weight, neighbours, innovation, obs_type, live):
    ncol, nlev = lax.axis_size("col"), lax.axis_size("lev")
    nlo = 2 if nlev % 2 == 0 else 1
    nhi = nlev // nlo
    levels, members, columns = state_anom.shape
    mq, obs_slots = obs_anom.shape
    neigh = local_weight.shape[0]
    quarter = innovation.shape[0]
    handled = quarter * nhi
    groups = LANES // neigh
    go = handled // groups
    half = nlo * mq
    depth = -(-3 * half // LANES) * LANES
    total = ncol * nlev
    chunks = 1 if columns % (2 * LANES) == 0 else 1
    width = columns // chunks
    dma = pltpu.SemaphoreType.DMA
    f32, bf16, i32 = jnp.float32, jnp.bfloat16, jnp.int32
    vm = pltpu.VMEM
    scratch = [
        vm((levels, members, columns), bf16), vm((levels, columns), f32), vm((nlev, mq, columns), f32),
        vm((max(nlev - 1, 1), mq, columns), f32), vm((3, nlo, mq, columns), f32), vm((nlo, mq, handled), bf16),
        vm((handled, depth), bf16), vm((LANES, go), f32), vm((LANES, go), i32), vm((go, LANES), i32),
        vm((nhi, 1, quarter), f32), vm((nhi, 1, quarter), i32), vm((nhi, 1, quarter), i32),
        vm((depth, width), bf16), vm((groups, go, width), f32), vm((go, LANES), f32),
        vm((nhi, 1, quarter), f32), vm((max(nhi - 1, 1), 1, quarter), f32),
        vm((1, LANES), f32), vm((total, 1, LANES), f32),
        pltpu.SemaphoreType.REGULAR((max(1, (ncol - 1).bit_length()),)),
        dma((1,)), dma((chunks,)), dma((2, groups)), dma((nhi,)), dma((3,)),
        dma((nlev, chunks)), dma((nlev, chunks)), dma((nlo, nhi)), dma((nlo, nhi)), dma((nhi, 3)), dma((nhi, 3)),
        dma((nlo, chunks)), dma((nlo, chunks)), dma((2, chunks)), dma((2, chunks)),
        dma((nlo, 3, chunks)), dma((nlo, 3, chunks)),
        dma((nhi,)), dma((nhi,)), dma((1,)), dma((1,)),
    ]
    anywhere = pl.BlockSpec(memory_space=pl.ANY)
    impact, totals = pl.pallas_call(
        functools.partial(kernel, (ncol, nlev, nlo, nhi, groups, chunks)),
        out_shape=(jax.ShapeDtypeStruct((1, quarter), f32), jax.ShapeDtypeStruct((1, LANES), f32)),
        in_specs=[anywhere] * 8,
        out_specs=(pl.BlockSpec(memory_space=pltpu.VMEM), pl.BlockSpec(memory_space=pltpu.VMEM)),
        scratch_shapes=scratch,
        compiler_params=pltpu.CompilerParams(collective_id=0, has_side_effects=True),
    )(
        state_anom, error_sum, obs_anom, local_weight, neighbours,
        innovation.reshape(1, quarter), obs_type.reshape(1, quarter), live.reshape(1, quarter),
    )
    impact, totals = pl.pallas_call(
        hand_over, out_shape=(jax.ShapeDtypeStruct((1, quarter), f32), jax.ShapeDtypeStruct((1, NTYPE), f32))
    )(impact, totals)
    return impact.reshape(quarter), totals.reshape(NTYPE)


def solution(mesh):
    in_specs = (
        P("lev", None, "col"),
        P("lev", "col"),
        P("lev", "col"),
        P(None, "col"),
        P(None, "col"),
        P(("col", "lev")),
        P(("col", "lev")),
        P(("col", "lev")),
    )
    out_specs = (P(("col", "lev")), P())
    return jax.shard_map(shards, mesh=mesh, in_specs=in_specs, out_specs=out_specs, check_vma=False)
```
